32 devices in a mesh: user: 4 (over y, x), seq: 8 (over z, core).
Axes of the slice: x: 2, y: 2, z: 4, core: 2. Of those that a mesh axis runs over, the one named last changes fastest.
Arguments:
- events: bfloat16 [16384, 1024], P(('user', 'seq')), may hold values from -6 to 6
- routing: int32 [128, 1], P(('user', 'seq')), may hold values from 0 to 3; in each aligned block of 4 rows (0 to 3, 4 to 7, ...) at most 2 rows name the same one
- grad_out: bfloat16 [4, 8192, 1024], P('user', 'seq'), may hold values from -6 to 6
- w_query: bfloat16 [1024, 1024], replicated, may hold values from -0.1875 to 0.1875
- w_key: bfloat16 [1024, 1024], replicated, may hold values from -0.1875 to 0.1875
- w_value: bfloat16 [1024, 1024], replicated, may hold values from -0.1875 to 0.1875
Outputs:
- grad_events: bfloat16 [16384, 1024], P(('user', 'seq'))
- grad_wq: float32 [1024, 1024], P(('user', 'seq'))
- grad_wk: float32 [1024, 1024], P(('user', 'seq'))
- grad_wv: float32 [1024, 1024], P(('user', 'seq'))
The draws below stay inside these ranges and needn't reach their ends.
Inputs may be any that keep to these rules, and one draw needn't show every extreme that they name: `routing`: among the 4 blocks of one device at most 2 have the same value.
All inputs are finite; a program needn't handle non-finite values.
Results may differ from the reference program's by a relative error of at most 0.015.
Values may be sent and summed in bfloat16 or wider, within the bound.
A program may use at most 192 MiB of HBM per device.

```python
import math
import jax
import jax.numpy as jnp
import numpy as np
from jax import lax

D = 1024
HEAD = 128
EVB = 128
WINDOW = 512
BLK_DEV = 4
CAP = 2
HIST = 8192
USERS = 4
EVENTS = 16384
NBLOCKS = 128
N_USER = 4
N_SEQ = 8


def block_scale(stream_key, shape, cuts, low, high):
    loudness, own = 1.0, jax.random.fold_in(stream_key, 6)
    for position, blocks in cuts:
        steps = jnp.exp(jax.random.uniform(jax.random.fold_in(own, position), (blocks,), jnp.float32, low / len(cuts), high / len(cuts)))
        loudness = loudness * jnp.repeat(steps, shape[position] // blocks).reshape([-1 if axis == position else 1 for axis in range(len(shape))])
    return loudness


def shared_out(own_key, own, number, rows, count, top, bound, lean):
    order = jax.random.permutation(own_key, count)
    crowded, ordinary = load_shares(count, rows * top, bound, lean, True), load_shares(count, rows * top, bound, lean, False)
    places = jnp.arange(count)

    def named(sizes, rotation):
        used = int((sizes > 0).sum())
        fixed = max(1, used // 4)
        moved = fixed + (places - fixed + rotation * (used - fixed)) % max(1, count - fixed)
        return jnp.zeros((count,), jnp.int32).at[order[jnp.where(places < fixed, places, moved)]].set(jnp.asarray(sizes, jnp.int32))

    sizes = jnp.where(number % 4 == 0, named(crowded, number // 4), named(ordinary, number - number // 4 - 1))
    mixed = jax.random.permutation(jax.random.fold_in(own, 3), count)
    donor, receiver = mixed[0:count // 2 * 2:2], mixed[1:count // 2 * 2:2]
    slack = jnp.minimum(sizes[donor] - 1, bound - sizes[receiver]) // 2
    slack = jnp.where((donor == order[0]) | (receiver == order[0]) | (sizes[receiver] == 0), 0, jnp.maximum(slack, 0))
    moved = jax.random.randint(jax.random.fold_in(own, 4), (count // 2,), 0, 1 << 20) % (slack + 1)
    sizes = sizes.at[donor].add(-moved).at[receiver].add(moved)
    members = jnp.searchsorted(jnp.cumsum(sizes), jnp.arange(rows * top), side="right").astype(jnp.int32)
    listing = members.reshape(top, rows).T
    listing = listing[jax.random.permutation(jax.random.fold_in(own, 1), rows)]
    rotation = jax.random.randint(jax.random.fold_in(own, 2), (rows, 1), 0, top)
    return jnp.take_along_axis(listing, (jnp.arange(top)[None, :] + rotation) % top, axis=1)


def load_shares(number_of, total, bound, slope, full):
    weights = [(1 << 20) // math.isqrt(grade ** slope) + 1 for grade in range(1, number_of + 1)]
    largest = bound if full else min(bound, max(-(-total // number_of), total * weights[0] // sum(weights)))
    least = 1 if total - largest >= number_of - 1 else 0
    holding, surplus = [largest] + [least] * (number_of - 1), total - largest - least * (number_of - 1)
    while surplus > 0:
        movable = [i for i in range(1, number_of) if holding[i] < largest] or [i for i in range(1, number_of) if holding[i] < bound]
        mass, left = sum([weights[i] for i in movable]), surplus
        for i in movable:
            addition = min(bound - holding[i], max(1, left * weights[i] // mass), surplus)
            holding[i] = holding[i] + addition
            surplus = surplus - addition
    return np.array(holding)


def noise(key, extent, width, bound, split=(), kind=jnp.bfloat16):
    result = jax.random.normal(key, extent, jnp.float32) * width
    if len(split) > 0:
        result = block_scale(key, extent, split, -0.22, 0.18) * result
    return jnp.clip(result, min=-bound, max=bound).astype(kind)


def setup_inputs(seed: int = 0) -> dict:
    seeds = jax.random.split(jax.random.key(seed), 7)
    events = noise(seeds[0], (EVENTS, D), 1.0, 6.0, ((0, 32),))
    routing_keys = jax.random.split(jax.random.fold_in(seeds[1], 1), NBLOCKS // BLK_DEV)
    routing_turns = jax.random.permutation(jax.random.fold_in(seeds[1], 3), NBLOCKS // BLK_DEV)
    routing = jax.vmap(lambda own, number: shared_out(jax.random.fold_in(seeds[1], 2), own, number, BLK_DEV, N_USER, 1, CAP, 2))(routing_keys, routing_turns).reshape((NBLOCKS, 1))
    grad_out = noise(seeds[2], (USERS, HIST, D), 1.0, 6.0, ((0, 4), (1, 8)))
    w_query = noise(seeds[3], (D, D), D ** -0.5, 0.1875)
    w_key = noise(seeds[4], (D, D), D ** -0.5, 0.1875)
    w_value = noise(seeds[5], (D, D), D ** -0.5, 0.1875)
    return dict(events=events, routing=routing, grad_out=grad_out, w_query=w_query, w_key=w_key, w_value=w_value)


def pick_table(route_col, users, capacity):
    count = route_col.shape[0]
    order = jnp.arange(count, dtype=jnp.int32)
    same_dest = route_col[None, :] == route_col[:, None]
    earlier = order[None, :] < order[:, None]
    ranking = lax.optimization_barrier(jnp.sum((same_dest & earlier).astype(jnp.int32), axis=1))
    slot_ids = jnp.arange(users * capacity, dtype=jnp.int32)
    chosen = (route_col[None, :] == (slot_ids // capacity)[:, None]) & (ranking[None, :] == (slot_ids % capacity)[:, None])
    return chosen.astype(jnp.bfloat16)

def to_float(array):
    return array.astype(jnp.float32)

def rounded(array):
    return to_float(lax.optimization_barrier(array.astype(jnp.bfloat16)))

def reference(events, routing, grad_out, w_query, w_key, w_value):
    devices = N_USER * N_SEQ
    highest = lax.Precision.HIGHEST
    blocks_all = events.reshape(devices, BLK_DEV, EVB * D)
    routes_all = routing.reshape(devices, BLK_DEV)
    tables = lax.map(lambda route_col: pick_table(route_col, N_USER, CAP), routes_all)
    packed = lax.map(lambda pair: jnp.dot(pair[0], pair[1], preferred_element_type=jnp.float32).astype(jnp.bfloat16), (tables, blocks_all))
    packed = packed.reshape(N_USER, N_SEQ, N_USER, CAP * EVB, D)
    history = jnp.transpose(packed, (2, 1, 0, 3, 4)).reshape(N_USER, HIST, D)
    heads = D // HEAD
    nwin = HIST // WINDOW
    scale = 1.0 / math.sqrt(HEAD * HIST)
    lower = jnp.arange(WINDOW)[None, :] <= jnp.arange(WINDOW)[:, None]

    def user_grads(pair):
        rows_in, upstream = pair
        shape4 = (nwin, WINDOW, heads, HEAD)
        queries = jnp.dot(rows_in, w_query, preferred_element_type=jnp.float32).astype(jnp.bfloat16).reshape(shape4)
        key_rows = jnp.dot(rows_in, w_key, preferred_element_type=jnp.float32).astype(jnp.bfloat16).reshape(shape4)
        value_rows = jnp.dot(rows_in, w_value, preferred_element_type=jnp.float32).astype(jnp.bfloat16).reshape(shape4)
        cot_rows = upstream.reshape(shape4)
        kv_win = jnp.einsum('wjhk,wjhv->whkv', to_float(key_rows), to_float(value_rows), precision=highest)
        qd_win = jnp.einsum('wihq,wiho->whqo', to_float(queries), to_float(cot_rows), precision=highest)
        before = jnp.cumsum(kv_win, 0) - kv_win
        after = lax.optimization_barrier(jnp.sum(qd_win, 0))[None] - jnp.cumsum(qd_win, 0)

        def window(items):
            q_win, k_win, v_win, o_win, b_win, a_win = [to_float(item) for item in items[:4]] + list(items[4:])
            before_b = rounded(b_win)
            after_b = rounded(a_win)
            attn = jnp.einsum('ihd,jhd->hij', q_win, k_win, precision=highest)
            mixes = jnp.einsum('ihd,jhd->hij', o_win, v_win, precision=highest)
            attn_b = rounded(jnp.where(lower[None], attn, 0.0))
            mixes_b = rounded(jnp.where(lower[None], mixes, 0.0))
            grad_q = scale * (jnp.einsum('hij,jhd->ihd', mixes_b, k_win, precision=highest) + jnp.einsum('ihe,hde->ihd', o_win, before_b, precision=highest))
            grad_k = scale * (jnp.einsum('hij,ihd->jhd', mixes_b, q_win, precision=highest) + jnp.einsum('jhe,hde->jhd', v_win, after_b, precision=highest))
            grad_v = scale * (jnp.einsum('hij,ihd->jhd', attn_b, o_win, precision=highest) + jnp.einsum('jhd,hde->jhe', k_win, after_b, precision=highest))
            return (grad_q.astype(jnp.bfloat16), grad_k.astype(jnp.bfloat16), grad_v.astype(jnp.bfloat16))
        grad_q, grad_k, grad_v = lax.map(window, (queries, key_rows, value_rows, cot_rows, before, after))
        grad_q = grad_q.reshape(HIST, D)
        grad_k = grad_k.reshape(HIST, D)
        grad_v = grad_v.reshape(HIST, D)
        dims = (((1,), (1,)), ((), ()))
        grad_hist = lax.dot_general(grad_q, w_query, dims, preferred_element_type=jnp.float32)
        grad_hist = grad_hist + lax.dot_general(grad_k, w_key, dims, preferred_element_type=jnp.float32)
        grad_hist = grad_hist + lax.dot_general(grad_v, w_value, dims, preferred_element_type=jnp.float32)
        grads = jnp.concatenate([grad_q, grad_k, grad_v], axis=1)
        weight_term = lax.dot_general(rows_in, grads, (((0,), (0,)), ((), ())), preferred_element_type=jnp.float32)
        return (grad_hist.astype(jnp.bfloat16), weight_term)
    grad_hist, terms = lax.map(user_grads, (history, grad_out))
    factor = 1.0 / math.sqrt(N_USER * HIST)
    weights = lax.optimization_barrier(jnp.sum(terms, axis=0)) * factor
    back = grad_hist.reshape(N_USER, N_SEQ, N_USER, CAP * EVB, D)
    back = jnp.transpose(back, (2, 1, 0, 3, 4)).reshape(devices, N_USER * CAP, EVB * D)
    grad_events = lax.map(lambda pair: jnp.dot(pair[0].T, pair[1], preferred_element_type=jnp.float32).astype(jnp.bfloat16), (tables, back))
    grad_events = grad_events.reshape(EVENTS, D)
    return (grad_events, weights[:, :D], weights[:, D:2 * D], weights[:, 2 * D:])
```

```python
import functools
import math

import jax
import jax.numpy as jnp
from jax import lax
from jax.experimental import pallas as pl
from jax.experimental.pallas import tpu as pltpu
from jax.sharding import PartitionSpec as P

HEAD = 128
EVB = 128
WINDOW = 512
PAIR = 2 * HEAD
F32 = jnp.float32
BF16 = jnp.bfloat16
NT = (((1,), (1,)), ((), ()))
TN = (((0,), (0,)), ((), ()))
VMEM_LIMIT = 56 * 1024 * 1024


def mm(a, b):
    return jnp.dot(a, b, preferred_element_type=F32)


def mm_nt(a, b):
    return lax.dot_general(a, b, NT, preferred_element_type=F32)


def cost(flops, nbytes):
    return pl.CostEstimate(flops=flops, bytes_accessed=nbytes, transcendentals=0)


def params(semantics=("arbitrary",)):
    return pltpu.CompilerParams(dimension_semantics=semantics, vmem_limit_bytes=VMEM_LIMIT)


def gather_blocks(source, index, valid, rows):
    width = source.shape[-1]

    def body(index_ref, valid_ref, src, out):
        keep = valid_ref[pl.program_id(0)] > 0

        @pl.when(keep)
        def _():
            out[...] = src[...]

        @pl.when(jnp.logical_not(keep))
        def _():
            out[...] = jnp.zeros_like(out)

    return pl.pallas_call(
        body,
        out_shape=jax.ShapeDtypeStruct((rows, EVB, width), source.dtype),
        grid_spec=pltpu.PrefetchScalarGridSpec(
            num_scalar_prefetch=2,
            grid=(rows,),
            in_specs=[pl.BlockSpec((1, EVB, width), lambda i, ix, va: (ix[i], 0, 0))],
            out_specs=pl.BlockSpec((1, EVB, width), lambda i, ix, va: (i, 0, 0)),
        ),
        compiler_params=params(),
        cost_estimate=cost(0, 4 * rows * EVB * width),
    )(index, valid, source)


def project(me, pieces, cot, w_query, w_key, w_value):
    users = len(pieces)
    part, width = pieces[0].shape
    slots = users * part
    nwin = slots // WINDOW
    heads = width // HEAD

    def body(me_ref, *refs):
        parts = refs[:users]
        cot_ref, wq, wk, wv = refs[users : users + 4]
        hist, q_ref, k_ref, v_ref, kvw, qdw, st = refs[users + 4 :]

        @pl.when(pl.program_id(0) == 0)
        def _():
            for j in range(users):
                at = pl.multiple_of(jnp.bitwise_xor(me_ref[0], j) * part, part)
                hist[pl.ds(at, part), :] = parts[j][...]

        kv_sum = [0.0, 0.0]
        qd_sum = [0.0, 0.0]
        for w in range(nwin):
            rows = pl.ds(w * WINDOW, WINDOW)
            h = hist[rows, :]
            q = mm(h, wq[...]).astype(BF16)
            k = mm(h, wk[...]).astype(BF16)
            v = mm(h, wv[...]).astype(BF16)
            q_ref[rows, :] = q
            k_ref[rows, :] = k
            v_ref[rows, :] = v
            o = cot_ref[rows, :]
            kv = lax.dot_general(k, v, TN, preferred_element_type=F32)
            qd = lax.dot_general(q, o, TN, preferred_element_type=F32)
            for h in range(2):
                sl = slice(h * HEAD, (h + 1) * HEAD)
                kvw[w, h] = kv[sl, sl]
                qdw[w, h] = qd[sl, sl]
                kv_sum[h] = kv_sum[h] + kv[sl, sl]
                qd_sum[h] = qd_sum[h] + qd[sl, sl]
        for h in range(2):
            st[0, h] = kv_sum[h].astype(BF16)
            st[1, h] = qd_sum[h].astype(BF16)

    col = pl.BlockSpec((slots, PAIR), lambda i, m: (0, i))
    wspec = pl.BlockSpec((width, PAIR), lambda i, m: (0, i))
    win = pl.BlockSpec((nwin, 2, HEAD, HEAD), lambda i, m: (0, i, 0, 0))
    act = jax.ShapeDtypeStruct((slots, width), BF16)
    state = jax.ShapeDtypeStruct((nwin, heads, HEAD, HEAD), F32)
    return pl.pallas_call(
        body,
        out_shape=(
            act,
            act,
            act,
            act,
            state,
            state,
            jax.ShapeDtypeStruct((2, heads, HEAD, HEAD), BF16),
        ),
        grid_spec=pltpu.PrefetchScalarGridSpec(
            num_scalar_prefetch=1,
            grid=(width // PAIR,),
            in_specs=[pl.BlockSpec((part, width), lambda i, m: (0, 0))] * users
            + [col, wspec, wspec, wspec],
            out_specs=(
                pl.BlockSpec((slots, width), lambda i, m: (0, 0)),
                col,
                col,
                col,
                win,
                win,
                pl.BlockSpec((2, 2, HEAD, HEAD), lambda i, m: (0, i, 0, 0)),
            ),
        ),
        compiler_params=params(),
        cost_estimate=cost(6 * slots * width * width, 18 * slots * width),
    )(me, *pieces, cot, w_query, w_key, w_value)


def intra(which, q, k, v, cot):
    width = q.shape[1]
    half = WINDOW // 2

    def body(q_ref, k_ref, v_ref, o_ref, iq, ik, iv):
        row = lax.broadcasted_iota(jnp.int32, (half, half), 0)
        lane = lax.broadcasted_iota(jnp.int32, (half, half), 1)
        low = lane <= row
        high = lane >= row
        a, b = slice(0, half), slice(half, WINDOW)

        def masked(x, keep):
            return jnp.where(keep, x, 0.0).astype(BF16)

        for h in range(2):
            sl = slice(h * HEAD, (h + 1) * HEAD)
            q, k, v, o = q_ref[:, sl], k_ref[:, sl], v_ref[:, sl], o_ref[:, sl]
            iq[a, sl] = mm(masked(mm_nt(o[a], v[a]), low), k[a])
            m10 = mm_nt(o[b], v[a]).astype(BF16)
            m11 = masked(mm_nt(o[b], v[b]), low)
            iq[b, sl] = mm(m10, k[a]) + mm(m11, k[b])
            t00 = masked(mm_nt(v[a], o[a]), high)
            t01 = mm_nt(v[a], o[b]).astype(BF16)
            ik[a, sl] = mm(t00, q[a]) + mm(t01, q[b])
            ik[b, sl] = mm(masked(mm_nt(v[b], o[b]), high), q[b])
            s00 = masked(mm_nt(k[a], q[a]), high)
            s01 = mm_nt(k[a], q[b]).astype(BF16)
            iv[a, sl] = mm(s00, o[a]) + mm(s01, o[b])
            iv[b, sl] = mm(masked(mm_nt(k[b], q[b]), high), o[b])

    col = pl.BlockSpec((WINDOW, PAIR), lambda i: (which, i))
    out = pl.BlockSpec((WINDOW, PAIR), lambda i: (0, i))
    return pl.pallas_call(
        body,
        out_shape=(jax.ShapeDtypeStruct((WINDOW, width), F32),) * 3,
        grid=(width // PAIR,),
        in_specs=[col] * 4,
        out_specs=(out,) * 3,
        compiler_params=params(),
        cost_estimate=cost(18 * WINDOW * WINDOW * width, 20 * WINDOW * width),
    )(q, k, v, cot)


def finish(core, scale, factor, groups, parts, k, v, cot, hist, before, after):
    slots, width = k.shape
    nwin = len(parts)
    own = width // (2 * groups)

    def body(core_ref, *refs):
        inner = [refs[3 * w : 3 * w + 3] for w in range(nwin)]
        k_ref, v_ref, o_ref, h_ref, b_ref, a_ref = refs[3 * nwin : 3 * nwin + 6]
        outs = refs[3 * nwin + 6 : 3 * nwin + 9]
        keep, send, ht, acc = refs[3 * nwin + 9 :]

        @pl.when(pl.program_id(0) == 0)
        def _():
            ht[...] = h_ref[...].T

        for w in range(nwin):
            rows = slice(w * WINDOW, (w + 1) * WINDOW)
            for h in range(2):
                sl = slice(h * HEAD, (h + 1) * HEAD)
                bef, aft = b_ref[w, h], a_ref[w, h]
                gq = inner[w][0][:, sl] + mm_nt(o_ref[rows, sl], bef)
                gk = inner[w][1][:, sl] + mm_nt(v_ref[rows, sl], aft)
                gv = inner[w][2][:, sl] + mm(k_ref[rows, sl], aft)
                for out, g in zip(outs, (gq, gk, gv)):
                    out[rows, sl] = (g * scale).astype(BF16)
        mine = core_ref[0]
        for n in range(3):
            acc[...] = mm(ht[...], outs[n][...]) * factor
            for g in range(groups):
                at = pl.multiple_of(g * 2 * own + mine * own, 8)
                away = pl.multiple_of(g * 2 * own + (1 - mine) * own, 8)
                keep[n, g] = acc[pl.ds(at, own), :].astype(BF16)
                send[n, g] = acc[pl.ds(away, own), :].astype(BF16)

    piece = pl.BlockSpec((WINDOW, PAIR), lambda i, c: (0, i))
    col = pl.BlockSpec((slots, PAIR), lambda i, c: (0, i))
    win = pl.BlockSpec((nwin, 2, HEAD, HEAD), lambda i, c: (0, i, 0, 0))
    wout = pl.BlockSpec((3, groups, own, PAIR), lambda i, c: (0, 0, 0, i))
    act = jax.ShapeDtypeStruct((slots, width), BF16)
    wshape = jax.ShapeDtypeStruct((3, groups, own, width), BF16)
    return pl.pallas_call(
        body,
        out_shape=(act, act, act, wshape, wshape),
        grid_spec=pltpu.PrefetchScalarGridSpec(
            num_scalar_prefetch=1,
            grid=(width // PAIR,),
            in_specs=[piece] * (3 * nwin)
            + [col, col, col, pl.BlockSpec((slots, width), lambda i, c: (0, 0)), win, win],
            out_specs=(col, col, col, wout, wout),
            scratch_shapes=[
                pltpu.VMEM((width, slots), BF16),
                pltpu.VMEM((width, PAIR), F32),
            ],
        ),
        compiler_params=params(),
        cost_estimate=cost(6 * slots * width * width, 30 * slots * width),
    )(core, *[x for p in parts for x in p], k, v, cot, hist, before, after)


def to_history(me, users, grads, weights):
    slots, width = grads[0].shape
    part = slots // users

    def body(me_ref, gq, gk, gv, wq, wk, wv, out):
        total = mm_nt(gq[...], wq[...]) + mm_nt(gk[...], wk[...])
        out[0] = (total + mm_nt(gv[...], wv[...])).astype(BF16)

    rows = pl.BlockSpec((part, width), lambda i, m: (jnp.bitwise_xor(m[0], i), 0))
    full = pl.BlockSpec((width, width), lambda i, m: (0, 0))
    return pl.pallas_call(
        body,
        out_shape=jax.ShapeDtypeStruct((users, part, width), BF16),
        grid_spec=pltpu.PrefetchScalarGridSpec(
            num_scalar_prefetch=1,
            grid=(users,),
            in_specs=[rows] * 3 + [full] * 3,
            out_specs=pl.BlockSpec((1, part, width), lambda i, m: (i, 0, 0)),
        ),
        compiler_params=params(),
        cost_estimate=cost(6 * slots * width * width, 14 * slots * width),
    )(me, *grads, *weights)


def swap(x, axis, size, bits):
    return lax.ppermute(x, axis, [(i, i ^ bits) for i in range(size)])


def shift(x, axis, size, by):
    return lax.ppermute(x, axis, [(i, i + by) for i in range(size) if 0 <= i + by < size])


def add(*terms):
    return functools.reduce(jnp.add, [t.astype(F32) for t in terms])


def pick(x, index, axis):
    return lax.dynamic_index_in_dim(x, index, axis, keepdims=False)


def carried(state, shards, core):
    chips = shards // 2
    half = state.shape[1] // 2
    other = swap(state, "seq", shards, 1)
    mine = add(
        lax.dynamic_slice_in_dim(state, core * half, half, 1),
        lax.dynamic_slice_in_dim(other, core * half, half, 1),
    ).astype(BF16)
    kv = add(*[shift(mine[0], "seq", shards, 2 * j) for j in range(1, chips)])
    qd = add(*[shift(mine[1], "seq", shards, -2 * j) for j in range(1, chips)])
    sums = jnp.stack([kv, qd]).astype(BF16)
    theirs = swap(sums, "seq", shards, 1)
    first = core == 0
    whole = jnp.concatenate(
        [jnp.where(first, sums, theirs), jnp.where(first, theirs, sums)], axis=1
    ).astype(F32)
    prior = whole[0] + jnp.where(first, 0.0, other[0].astype(F32))
    later = whole[1] + jnp.where(first, other[1].astype(F32), 0.0)
    return prior, later


def scatter_sums(keep, send, users, shards, me, place):
    chips = shards // 2
    own, width = keep.shape[2:]
    low, high = me % 2, me // 2
    z = place // 2
    got = swap(send, "seq", shards, 1)
    shape = (3, users // 2, 2, chips, own, width)
    halves = []
    for side in range(2):
        cols = slice(side * (width // 2), (side + 1) * (width // 2))
        a, b = keep.reshape(shape)[..., cols], got.reshape(shape)[..., cols]
        axis, at, bit = (2, low, 1) if side == 0 else (1, high, 2)
        away = add(pick(a, 1 - at, axis), pick(b, 1 - at, axis)).astype(BF16)
        here = add(pick(a, at, axis), pick(b, at, axis)).astype(BF16)
        came = swap(away, "user", users, bit)
        at, bit = (high, 2) if side == 0 else (low, 1)
        away = add(pick(here, 1 - at, 1), pick(came, 1 - at, 1)).astype(BF16)
        here = add(pick(here, at, 1), pick(came, at, 1)).astype(BF16)
        halves.append((here, swap(away, "user", users, bit)))

    def chunk(index):
        pieces = [add(pick(x, index, 1), pick(y, index, 1)) for x, y in halves]
        return jnp.concatenate(pieces, axis=-1)

    came = [
        swap(chunk(jnp.bitwise_xor(z, j)).astype(BF16), "seq", shards, 2 * j)
        for j in range(1, chips)
    ]
    return add(chunk(z), *came)


def local(events, routing, grad_out, w_query, w_key, w_value):
    users = lax.axis_size("user")
    shards = lax.axis_size("seq")
    me = lax.axis_index("user").astype(jnp.int32)
    place = lax.axis_index("seq").astype(jnp.int32)
    core = place % 2
    blocks = routing.shape[0]
    width = events.shape[1]
    slots = grad_out.shape[1]
    capacity = slots // (users * EVB)
    nwin = slots // WINDOW
    route = routing[:, 0]

    order = lax.iota(jnp.int32, blocks)
    same = (route[None, :] == route[:, None]) & (order[None, :] < order[:, None])
    rank = jnp.sum(same.astype(jnp.int32), axis=1)
    home = jnp.bitwise_xor(route, me) * capacity + rank
    slot = lax.iota(jnp.int32, users * capacity)
    hit = home[None, :] == slot[:, None]
    source = jnp.sum(jnp.where(hit, order[None, :], 0), axis=1)
    filled = jnp.sum(hit.astype(jnp.int32), axis=1)
    me1, core1 = me.reshape(1), core.reshape(1)

    packed = gather_blocks(events.reshape(blocks, EVB, width), source, filled, users * capacity)
    packed = packed.reshape(users, capacity * EVB, width)
    pieces = [packed[0]] + [swap(packed[j], "user", users, j) for j in range(1, users)]
    cot = grad_out[0]
    hist, q, k, v, kv_win, qd_win, state = project(me1, pieces, cot, w_query, w_key, w_value)
    prior, later = carried(state, shards, core)
    parts = [intra(w, q, k, v, cot) for w in range(nwin)]
    before = (prior[None] + jnp.cumsum(kv_win, axis=0) - kv_win).astype(BF16)
    after = later[None] + jnp.sum(qd_win, axis=0)[None] - jnp.cumsum(qd_win, axis=0)
    after = after.astype(BF16)
    scale = 1.0 / math.sqrt(HEAD * slots * shards)
    factor = 1.0 / math.sqrt(users * slots * shards)
    groups = users * (shards // 2)
    gq, gk, gv, keep, send = finish(
        core1, scale, factor, groups, parts, k, v, cot, hist, before, after
    )
    back = to_history(me1, users, (gq, gk, gv), (w_query, w_key, w_value))
    returned = [back[0]] + [swap(back[j], "user", users, j) for j in range(1, users)]
    shares = scatter_sums(keep, send, users, shards, me, place)
    returned = jnp.concatenate(returned, axis=0).reshape(users * capacity, EVB, width)
    grad_events = gather_blocks(returned, home, jnp.ones_like(home), blocks)
    return (grad_events.reshape(blocks * EVB, width), shares[0], shares[1], shares[2])


def solution(mesh):
    placed = (
        P(("user", "seq"), None),
        P(("user", "seq"), None),
        P("user", "seq", None),
        P(),
        P(),
        P(),
    )
    return jax.shard_map(
        local,
        mesh=mesh,
        in_specs=placed,
        out_specs=(P(("user", "seq"), None),) * 4,
        check_vma=False,
    )
```

```python
import functools
import math

import jax
import jax.numpy as jnp
from jax import lax
from jax.experimental import pallas as pl
from jax.experimental.pallas import tpu as pltpu
from jax.sharding import PartitionSpec as P

HEAD = 128
EVB = 128
WINDOW = 512
PAIR = 2 * HEAD
F32 = jnp.float32
BF16 = jnp.bfloat16
NT = (((1,), (1,)), ((), ()))
TN = (((0,), (0,)), ((), ()))
VMEM_LIMIT = 56 * 1024 * 1024


def mm(a, b):
    return jnp.dot(a, b, preferred_element_type=F32)


def mm_nt(a, b):
    return lax.dot_general(a, b, NT, preferred_element_type=F32)


def cost(flops, nbytes):
    return pl.CostEstimate(flops=flops, bytes_accessed=nbytes, transcendentals=0)


def params(semantics=("arbitrary",)):
    return pltpu.CompilerParams(dimension_semantics=semantics, vmem_limit_bytes=VMEM_LIMIT)


def gather_blocks(source, index, valid, rows):
    width = source.shape[-1]

    def body(index_ref, valid_ref, src, out):
        keep = valid_ref[pl.program_id(0)] > 0

        @pl.when(keep)
        def _():
            out[...] = src[...]

        @pl.when(jnp.logical_not(keep))
        def _():
            out[...] = jnp.zeros_like(out)

    return pl.pallas_call(
        body,
        out_shape=jax.ShapeDtypeStruct((rows, EVB, width), source.dtype),
        grid_spec=pltpu.PrefetchScalarGridSpec(
            num_scalar_prefetch=2,
            grid=(rows,),
            in_specs=[pl.BlockSpec((1, EVB, width), lambda i, ix, va: (ix[i], 0, 0))],
            out_specs=pl.BlockSpec((1, EVB, width), lambda i, ix, va: (i, 0, 0)),
        ),
        compiler_params=params(),
        cost_estimate=cost(0, 4 * rows * EVB * width),
    )(index, valid, source)


MESH = pl.DeviceIdType.MESH


def project(packed, cot, weights, users):
    part, width = packed.shape[1:]
    slots = users * part
    heads = width // HEAD

    def body(src, cot_hbm, wq, wk, wv, hist, q_o, k_o, v_o, kvp, qdp, st, *scratch):
        buf, ws, cs, qs, ks, vs, total, send_sem, recv_sem, in_sem, out_sem = scratch
        me = lax.axis_index("user")
        barrier = pltpu.get_barrier_semaphore()
        for j in range(1, users):
            pl.semaphore_signal(
                barrier,
                inc=1,
                device_id={"user": jnp.bitwise_xor(me, j)},
                device_id_type=MESH,
            )
        pl.semaphore_wait(barrier, users - 1)
        remote = []
        for j in range(1, users):
            remote.append(
                pltpu.make_async_remote_copy(
                    src_ref=src.at[j],
                    dst_ref=buf.at[j],
                    send_sem=send_sem.at[j - 1],
                    recv_sem=recv_sem.at[j - 1],
                    device_id={"user": jnp.bitwise_xor(me, j)},
                    device_id_type=MESH,
                )
            )
            remote[-1].start()
        loads = [pltpu.make_async_copy(src.at[0], buf.at[0], in_sem.at[0])]
        for n, w in enumerate((wq, wk, wv)):
            loads.append(pltpu.make_async_copy(w, ws.at[n], in_sem.at[1 + n]))
        loads.append(pltpu.make_async_copy(cot_hbm, cs, in_sem.at[4]))
        for load in loads:
            load.start()
        total[...] = jnp.zeros_like(total)
        outs = []
        for j in range(users):
            if j == 0:
                for load in loads:
                    load.wait()
            else:
                remote[j - 1].wait_recv()
            at = pl.multiple_of(jnp.bitwise_xor(me, j) * part, part)
            rows = pl.ds(at, part)
            outs.append(pltpu.make_async_copy(buf.at[j], hist.at[rows], out_sem.at[j, 0]))
            outs[-1].start()

            def columns(c, carry, j=j, rows=rows):
                cols = pl.ds(pl.multiple_of(c * PAIR, PAIR), PAIR)
                h = buf[j]
                q = mm(h, ws[0, :, cols]).astype(BF16)
                k = mm(h, ws[1, :, cols]).astype(BF16)
                v = mm(h, ws[2, :, cols]).astype(BF16)
                qs[j, :, cols] = q
                ks[j, :, cols] = k
                vs[j, :, cols] = v
                o = cs[rows, cols]
                kv = lax.dot_general(k, v, TN, preferred_element_type=F32)
                qd = lax.dot_general(q, o, TN, preferred_element_type=F32)
                for i in range(2):
                    sl = slice(i * HEAD, (i + 1) * HEAD)
                    kvp[j, 2 * c + i] = kv[sl, sl]
                    qdp[j, 2 * c + i] = qd[sl, sl]
                    total[0, 2 * c + i] += kv[sl, sl]
                    total[1, 2 * c + i] += qd[sl, sl]
                return carry

            lax.fori_loop(0, width // PAIR, columns, 0)
            for n, (a, b) in enumerate(((qs, q_o), (ks, k_o), (vs, v_o))):
                outs.append(pltpu.make_async_copy(a.at[j], b.at[rows], out_sem.at[j, 1 + n]))
                outs[-1].start()
        st[...] = total[...].astype(BF16)
        for copy in outs:
            copy.wait()
        for copy in remote:
            copy.wait_send()

    anywhere = pl.BlockSpec(memory_space=pl.ANY)
    vmem = pl.BlockSpec(memory_space=pltpu.VMEM)
    act = jax.ShapeDtypeStruct((slots, width), BF16)
    state = jax.ShapeDtypeStruct((users, heads, HEAD, HEAD), F32)
    tile = pltpu.VMEM((users, part, width), BF16)
    return pl.pallas_call(
        body,
        out_shape=(
            act,
            act,
            act,
            act,
            state,
            state,
            jax.ShapeDtypeStruct((2, heads, HEAD, HEAD), BF16),
        ),
        in_specs=[anywhere] * 5,
        out_specs=(anywhere,) * 4 + (vmem,) * 3,
        scratch_shapes=[
            tile,
            pltpu.VMEM((3, width, width), BF16),
            pltpu.VMEM((slots, width), BF16),
            tile,
            tile,
            tile,
            pltpu.VMEM((2, heads, HEAD, HEAD), F32),
            pltpu.SemaphoreType.DMA((users - 1,)),
            pltpu.SemaphoreType.DMA((users - 1,)),
            pltpu.SemaphoreType.DMA((5,)),
            pltpu.SemaphoreType.DMA((users, 4)),
        ],
        compiler_params=pltpu.CompilerParams(
            collective_id=0, has_side_effects=True, vmem_limit_bytes=VMEM_LIMIT
        ),
        cost_estimate=cost(6 * slots * width * width, 18 * slots * width),
    )(packed, cot, *weights)


def gradients(q, k, v, cot, hist, kvp, qdp, st, users, shards, scale, factor):
    slots, width = q.shape
    heads = width // HEAD
    pairs = width // PAIR
    nwin = slots // WINDOW
    per_window = users // nwin
    chips = shards // 2
    half = heads // 2
    groups = users * chips
    own = width // (2 * groups)
    mid = WINDOW // 2

    def body(q_h, k_h, v_h, o_h, hist_h, kvp_h, qdp_h, st_ref, *refs):
        gq_o, gk_o, gv_o, sum_o = refs[:4]
        qs, ks, vs, os, hs, kvs, qds, oth, mine, rk, rq, tot, sums, theirs, states = refs[4:19]
        inner, gs, ht, acc, keep, send, got = refs[19:26]
        in_sem, far_sem, rk_sem, rq_sem, sk_sem, sq_sem, out_sem, ss_sem, gr_sem, so_sem = refs[26:]
        me = lax.axis_index("user")
        place = lax.axis_index("seq")
        core = place % 2
        z = place // 2
        mate = {"seq": place + 1 - 2 * core}

        def chip(by):
            return {"seq": ((z + by + chips) % chips) * 2 + core}

        loads = []
        for w in range(nwin):
            rows = pl.ds(w * WINDOW, WINDOW)
            loads.append(
                [
                    pltpu.make_async_copy(a.at[rows], b.at[rows], in_sem.at[w, n])
                    for n, (a, b) in enumerate(((q_h, qs), (k_h, ks), (v_h, vs), (o_h, os)))
                ]
            )
            for load in loads[-1]:
                load.start()
        late = [
            pltpu.make_async_copy(a, b, in_sem.at[nwin, n])
            for n, (a, b) in enumerate(((hist_h, hs), (kvp_h, kvs), (qdp_h, qds)))
        ]
        for load in late:
            load.start()

        barrier = pltpu.get_barrier_semaphore()
        pl.semaphore_signal(barrier, inc=1, device_id=mate, device_id_type=MESH)
        for j in range(1, chips):
            pl.semaphore_signal(barrier, inc=1, device_id=chip(j), device_id_type=MESH)
        pl.semaphore_wait(barrier, chips)
        swap_in = pltpu.make_async_remote_copy(
            src_ref=st_ref,
            dst_ref=oth,
            send_sem=far_sem.at[0],
            recv_sem=far_sem.at[1],
            device_id=mate,
            device_id_type=MESH,
        )
        swap_in.start()

        row = lax.broadcasted_iota(jnp.int32, (mid, mid), 0)
        lane = lax.broadcasted_iota(jnp.int32, (mid, mid), 1)

        def masked(x, keep_it):
            return jnp.where(keep_it, x, 0.0).astype(BF16)

        def inside(w, first, last):
            low = lane <= row
            high = lane >= row
            top, low_half = pl.ds(w * WINDOW, mid), pl.ds(w * WINDOW + mid, mid)

            def step(n, carry):
                cols = pl.ds(pl.multiple_of(n * HEAD, HEAD), HEAD)
                q0, q1 = qs[top, cols], qs[low_half, cols]
                k0, k1 = ks[top, cols], ks[low_half, cols]
                v0, v1 = vs[top, cols], vs[low_half, cols]
                o0, o1 = os[top, cols], os[low_half, cols]
                m00 = masked(mm_nt(o0, v0), low)
                m10 = mm_nt(o1, v0).astype(BF16)
                m11 = masked(mm_nt(o1, v1), low)
                t00 = masked(mm_nt(v0, o0), high)
                t01 = mm_nt(v0, o1).astype(BF16)
                t11 = masked(mm_nt(v1, o1), high)
                s00 = masked(mm_nt(k0, q0), high)
                s01 = mm_nt(k0, q1).astype(BF16)
                s11 = masked(mm_nt(k1, q1), high)
                inner[0, top, cols] = mm(m00, k0)
                inner[0, low_half, cols] = mm(m10, k0) + mm(m11, k1)
                inner[1, top, cols] = mm(t00, q0) + mm(t01, q1)
                inner[1, low_half, cols] = mm(t11, q1)
                inner[2, top, cols] = mm(s00, o0) + mm(s01, o1)
                inner[2, low_half, cols] = mm(s11, o1)
                return carry

            lax.fori_loop(first, last, step, 0)

        for load in loads[0]:
            load.wait()
        inside(0, 0, heads // 4)
        swap_in.wait()
        mine_heads = pl.ds(core * half, half)
        for n in range(2):
            both = st_ref[n, mine_heads].astype(F32) + oth[n, mine_heads].astype(F32)
            mine[n] = both.astype(BF16)
        inside(0, heads // 4, heads // 2)

        def far(kind, j):
            slots_in, send_s, recv_s = ((rk, sk_sem, rk_sem), (rq, sq_sem, rq_sem))[kind]
            return pltpu.make_async_remote_copy(
                src_ref=mine.at[kind],
                dst_ref=slots_in.at[j - 1],
                send_sem=send_s.at[j - 1],
                recv_sem=recv_s.at[j - 1],
                device_id=chip(j if kind == 0 else -j),
                device_id_type=MESH,
            )

        for j in range(1, chips):
            pl.when(z + j < chips)(lambda j=j: far(0, j).start())
            pl.when(z >= j)(lambda j=j: far(1, j).start())
        inside(0, heads // 2, heads)
        for w in range(1, nwin):
            for load in loads[w]:
                load.wait()
            inside(w, 0, heads - heads // 4 if w == nwin - 1 else heads)
        tot[...] = jnp.zeros_like(tot)
        for j in range(1, chips):

            @pl.when(z >= j)
            def _(j=j):
                far(0, j).wait_recv()
                tot[0] += rk[j - 1].astype(F32)
                far(1, j).wait_send()

            @pl.when(z + j < chips)
            def _(j=j):
                far(1, j).wait_recv()
                tot[1] += rq[j - 1].astype(F32)
                far(0, j).wait_send()

        sums[...] = tot[...].astype(BF16)
        inside(nwin - 1, heads - heads // 4, heads)
        swap_out = pltpu.make_async_remote_copy(
            src_ref=sums,
            dst_ref=theirs,
            send_sem=far_sem.at[2],
            recv_sem=far_sem.at[3],
            device_id=mate,
            device_id_type=MESH,
        )
        swap_out.start()
        for load in late:
            load.wait()
        ht[...] = hs[...].T
        swap_out.wait()
        other_heads = pl.ds((1 - core) * half, half)
        later_core = jnp.where(core == 1, 1.0, 0.0)
        for n in range(2):
            states[n, mine_heads] = tot[n]
            states[n, other_heads] = theirs[n].astype(F32)
            on = later_core if n == 0 else 1.0 - later_core
            states[n] = states[n] + on * oth[n].astype(F32)

        def push(c):
            return pltpu.make_async_remote_copy(
                src_ref=send.at[c],
                dst_ref=got.at[c],
                send_sem=ss_sem.at[c],
                recv_sem=gr_sem.at[c],
                device_id=mate,
                device_id_type=MESH,
            )

        def finish(c, carry):
            pl.when(c > 0)(lambda: push(c - 1).start())
            cols = pl.ds(pl.multiple_of(c * PAIR, PAIR), PAIR)
            for w in range(nwin):
                rows = pl.ds(w * WINDOW, WINDOW)
                for i in range(2):
                    head = 2 * c + i
                    at = pl.ds(pl.multiple_of(head * HEAD, HEAD), HEAD)
                    bef, aft = states[0, head], states[1, head]
                    for j in range(users):
                        its = jnp.bitwise_xor(me, j) // per_window
                        bef = bef + jnp.where(its < w, 1.0, 0.0) * kvs[j, head]
                        aft = aft + jnp.where(its > w, 1.0, 0.0) * qds[j, head]
                    bef, aft = bef.astype(BF16), aft.astype(BF16)
                    gq = inner[0, rows, at] + mm_nt(os[rows, at], bef)
                    gk = inner[1, rows, at] + mm_nt(vs[rows, at], aft)
                    gv = inner[2, rows, at] + mm(ks[rows, at], aft)
                    for n, g in enumerate((gq, gk, gv)):
                        gs[n, rows, at] = (g * scale).astype(BF16)
            for n in range(3):
                acc[...] = mm(ht[...], gs[n, :, cols]) * factor
                for g in range(groups):
                    at = pl.multiple_of(g * 2 * own + core * own, 8)
                    away = pl.multiple_of(g * 2 * own + (1 - core) * own, 8)
                    keep[c, n, g] = acc[pl.ds(at, own), :].astype(BF16)
                    send[c, n, g] = acc[pl.ds(away, own), :].astype(BF16)
            return carry

        lax.fori_loop(0, pairs, finish, 0)
        outs = [
            pltpu.make_async_copy(gs.at[n], g, out_sem.at[n])
            for n, g in enumerate((gq_o, gk_o, gv_o))
        ]
        for copy in outs:
            copy.start()

        def settle(c):
            push(c).wait()
            keep[c] = (keep[c].astype(F32) + got[c].astype(F32)).astype(BF16)
            return pltpu.make_async_copy(keep.at[c], sum_o.at[c], so_sem.at[c])

        for c in range(pairs):
            if c == min(1, pairs - 1):
                push(pairs - 1).start()
            settled = settle(c)
            settled.start()
            outs.append(settled)
        for copy in outs:
            copy.wait()

    anywhere = pl.BlockSpec(memory_space=pl.ANY)
    act = jax.ShapeDtypeStruct((slots, width), BF16)
    whole = pltpu.VMEM((slots, width), BF16)
    piece = pltpu.VMEM((users, heads, HEAD, HEAD), F32)
    pack = (pairs, 3, groups, own, PAIR)
    state = (2, heads, HEAD, HEAD)
    part = (2, half, HEAD, HEAD)
    one = pltpu.VMEM((chips - 1, half, HEAD, HEAD), BF16)
    sem = pltpu.SemaphoreType.DMA
    return pl.pallas_call(
        body,
        out_shape=(act, act, act, jax.ShapeDtypeStruct(pack, BF16)),
        in_specs=[anywhere] * 7 + [pl.BlockSpec(memory_space=pltpu.VMEM)],
        out_specs=(anywhere,) * 4,
        scratch_shapes=[
            whole,
            whole,
            whole,
            whole,
            whole,
            piece,
            piece,
            pltpu.VMEM(state, BF16),
            pltpu.VMEM(part, BF16),
            one,
            one,
            pltpu.VMEM(part, F32),
            pltpu.VMEM(part, BF16),
            pltpu.VMEM(part, BF16),
            pltpu.VMEM(state, F32),
            pltpu.VMEM((3, slots, width), F32),
            pltpu.VMEM((3, slots, width), BF16),
            pltpu.VMEM((width, slots), BF16),
            pltpu.VMEM((width, PAIR), F32),
            pltpu.VMEM(pack, BF16),
            pltpu.VMEM(pack, BF16),
            pltpu.VMEM(pack, BF16),
            sem((nwin + 1, 4)),
            sem((4,)),
            sem((chips - 1,)),
            sem((chips - 1,)),
            sem((chips - 1,)),
            sem((chips - 1,)),
            sem((3,)),
            sem((pairs,)),
            sem((pairs,)),
            sem((pairs,)),
        ],
        compiler_params=pltpu.CompilerParams(
            collective_id=1, has_side_effects=True, vmem_limit_bytes=VMEM_LIMIT
        ),
        cost_estimate=cost(12 * slots * width * width, 30 * slots * width),
    )(q, k, v, cot, hist, kvp, qdp, st)


def to_history(me, users, grads, weights):
    slots, width = grads[0].shape
    part = slots // users

    def body(me_ref, gq, gk, gv, wq, wk, wv, out):
        total = mm_nt(gq[...], wq[...]) + mm_nt(gk[...], wk[...])
        out[0] = (total + mm_nt(gv[...], wv[...])).astype(BF16)

    rows = pl.BlockSpec((part, width), lambda i, m: (jnp.bitwise_xor(m[0], i), 0))
    full = pl.BlockSpec((width, width), lambda i, m: (0, 0))
    return pl.pallas_call(
        body,
        out_shape=jax.ShapeDtypeStruct((users, part, width), BF16),
        grid_spec=pltpu.PrefetchScalarGridSpec(
            num_scalar_prefetch=1,
            grid=(users,),
            in_specs=[rows] * 3 + [full] * 3,
            out_specs=pl.BlockSpec((1, part, width), lambda i, m: (i, 0, 0)),
        ),
        compiler_params=params(),
        cost_estimate=cost(6 * slots * width * width, 14 * slots * width),
    )(me, *grads, *weights)


def swap(x, axis, size, bits):
    return lax.ppermute(x, axis, [(i, i ^ bits) for i in range(size)])


def add(*terms):
    return functools.reduce(jnp.add, [t.astype(F32) for t in terms])


def pick(x, index, axis):
    return lax.dynamic_index_in_dim(x, index, axis, keepdims=False)


def scatter_sums(sums, users, shards, me, place):
    chips = shards // 2
    pairs, _, _, own, width = sums.shape
    low, high = me % 2, me // 2
    z = place // 2
    split = sums.reshape(2, pairs // 2, 3, users // 2, 2, chips, own, width)
    halves = []
    for side in range(2):
        axis, at, bit = (3, low, 1) if side == 0 else (2, high, 2)
        away = pick(split[side], 1 - at, axis)
        here = pick(split[side], at, axis)
        came = swap(away, "user", users, bit)
        at, bit = (high, 2) if side == 0 else (low, 1)
        away = add(pick(here, 1 - at, 2), pick(came, 1 - at, 2)).astype(BF16)
        here = add(pick(here, at, 2), pick(came, at, 2)).astype(BF16)
        halves.append((here, swap(away, "user", users, bit)))

    def chunk(index):
        return jnp.concatenate([add(pick(x, index, 2), pick(y, index, 2)) for x, y in halves])

    came = [
        swap(chunk(jnp.bitwise_xor(z, j)).astype(BF16), "seq", shards, 2 * j)
        for j in range(1, chips)
    ]
    total = add(chunk(z), *came)
    return jnp.transpose(total, (1, 2, 0, 3)).reshape(3, own, pairs * width)


def local(events, routing, grad_out, w_query, w_key, w_value):
    users = lax.axis_size("user")
    shards = lax.axis_size("seq")
    me = lax.axis_index("user").astype(jnp.int32)
    place = lax.axis_index("seq").astype(jnp.int32)
    blocks = routing.shape[0]
    width = events.shape[1]
    slots = grad_out.shape[1]
    capacity = slots // (users * EVB)
    route = routing[:, 0]

    order = lax.iota(jnp.int32, blocks)
    same = (route[None, :] == route[:, None]) & (order[None, :] < order[:, None])
    rank = jnp.sum(same.astype(jnp.int32), axis=1)
    home = jnp.bitwise_xor(route, me) * capacity + rank
    slot = lax.iota(jnp.int32, users * capacity)
    hit = home[None, :] == slot[:, None]
    source = jnp.sum(jnp.where(hit, order[None, :], 0), axis=1)
    filled = jnp.sum(hit.astype(jnp.int32), axis=1)
    me1 = me.reshape(1)

    packed = gather_blocks(events.reshape(blocks, EVB, width), source, filled, users * capacity)
    packed = packed.reshape(users, capacity * EVB, width)
    cot = grad_out[0]
    weights = (w_query, w_key, w_value)
    hist, q, k, v, kvp, qdp, state = project(packed, cot, weights, users)
    scale = 1.0 / math.sqrt(HEAD * slots * shards)
    factor = 1.0 / math.sqrt(users * slots * shards)
    gq, gk, gv, sums = gradients(
        q, k, v, cot, hist, kvp, qdp, state, users, shards, scale, factor
    )
    back = to_history(me1, users, (gq, gk, gv), weights)
    returned = [back[0]] + [swap(back[j], "user", users, j) for j in range(1, users)]
    shares = scatter_sums(sums, users, shards, me, place)
    returned = jnp.concatenate(returned, axis=0).reshape(users * capacity, EVB, width)
    grad_events = gather_blocks(returned, home, jnp.ones_like(home), blocks)
    return (grad_events.reshape(blocks * EVB, width), shares[0], shares[1], shares[2])


def solution(mesh):
    placed = (
        P(("user", "seq"), None),
        P(("user", "seq"), None),
        P("user", "seq", None),
        P(),
        P(),
        P(),
    )
    return jax.shard_map(
        local,
        mesh=mesh,
        in_specs=placed,
        out_specs=(P(("user", "seq"), None),) * 4,
        check_vma=False,
    )
```

```python
import functools
import math

import jax
import jax.numpy as jnp
from jax import lax
from jax.experimental import pallas as pl
from jax.experimental.pallas import tpu as pltpu
from jax.sharding import PartitionSpec as P

HEAD = 128
EVB = 128
WINDOW = 512
PAIR = 2 * HEAD
F32 = jnp.float32
BF16 = jnp.bfloat16
NT = (((1,), (1,)), ((), ()))
TN = (((0,), (0,)), ((), ()))
VMEM_LIMIT = 56 * 1024 * 1024


def mm(a, b):
    return jnp.dot(a, b, preferred_element_type=F32)


def mm_nt(a, b):
    return lax.dot_general(a, b, NT, preferred_element_type=F32)


def cost(flops, nbytes):
    return pl.CostEstimate(flops=flops, bytes_accessed=nbytes, transcendentals=0)


def params(semantics=("arbitrary",)):
    return pltpu.CompilerParams(dimension_semantics=semantics, vmem_limit_bytes=VMEM_LIMIT)


MESH = pl.DeviceIdType.MESH


def project(events, source, filled, cot, weights, users):
    width = events.shape[-1]
    slots = cot.shape[0]
    part = slots // users
    capacity = part // EVB
    heads = width // HEAD

    def body(ev, from_ref, full_ref, cot_hbm, wq, wk, wv, hist, q_o, k_o, v_o, kvp, qdp, st, *scratch):
        src, buf, ws, cs, qs, ks, vs, total, send_sem, recv_sem, in_sem, out_sem = scratch
        me = lax.axis_index("user")
        loads = []
        for n, w in enumerate((wq, wk, wv)):
            loads.append(pltpu.make_async_copy(w, ws.at[n], in_sem.at[1 + n]))
        loads.append(pltpu.make_async_copy(cot_hbm, cs, in_sem.at[4]))
        for load in loads:
            load.start()
        for j in list(range(1, users)) + [0]:
            for c in range(capacity):
                n = j * capacity + c
                rows = ev[from_ref[n]]
                rows = jnp.where(full_ref[n] > 0, rows, jnp.zeros_like(rows))
                if j:
                    src[j, c * EVB : (c + 1) * EVB] = rows
                else:
                    buf[0, c * EVB : (c + 1) * EVB] = rows
        barrier = pltpu.get_barrier_semaphore()
        for j in range(1, users):
            pl.semaphore_signal(
                barrier,
                inc=1,
                device_id={"user": jnp.bitwise_xor(me, j)},
                device_id_type=MESH,
            )
        pl.semaphore_wait(barrier, users - 1)
        remote = []
        for j in range(1, users):
            remote.append(
                pltpu.make_async_remote_copy(
                    src_ref=src.at[j],
                    dst_ref=buf.at[j],
                    send_sem=send_sem.at[j - 1],
                    recv_sem=recv_sem.at[j - 1],
                    device_id={"user": jnp.bitwise_xor(me, j)},
                    device_id_type=MESH,
                )
            )
            remote[-1].start()
        total[...] = jnp.zeros_like(total)
        outs = []
        for j in range(users):
            if j == 0:
                for load in loads:
                    load.wait()
            else:
                remote[j - 1].wait_recv()
            at = pl.multiple_of(jnp.bitwise_xor(me, j) * part, part)
            rows = pl.ds(at, part)
            outs.append(pltpu.make_async_copy(buf.at[j], hist.at[rows], out_sem.at[j, 0]))
            outs[-1].start()

            def columns(c, carry, j=j, rows=rows):
                cols = pl.ds(pl.multiple_of(c * PAIR, PAIR), PAIR)
                h = buf[j]
                q = mm(h, ws[0, :, cols]).astype(BF16)
                k = mm(h, ws[1, :, cols]).astype(BF16)
                v = mm(h, ws[2, :, cols]).astype(BF16)
                qs[j, :, cols] = q
                ks[j, :, cols] = k
                vs[j, :, cols] = v
                o = cs[rows, cols]
                kv = lax.dot_general(k, v, TN, preferred_element_type=F32)
                qd = lax.dot_general(q, o, TN, preferred_element_type=F32)
                for i in range(2):
                    sl = slice(i * HEAD, (i + 1) * HEAD)
                    kvp[j, 2 * c + i] = kv[sl, sl]
                    qdp[j, 2 * c + i] = qd[sl, sl]
                    total[0, 2 * c + i] += kv[sl, sl]
                    total[1, 2 * c + i] += qd[sl, sl]
                return carry

            lax.fori_loop(0, width // PAIR, columns, 0)
            for n, (a, b) in enumerate(((qs, q_o), (ks, k_o), (vs, v_o))):
                outs.append(pltpu.make_async_copy(a.at[j], b.at[rows], out_sem.at[j, 1 + n]))
                outs[-1].start()
        st[...] = total[...].astype(BF16)
        for copy in outs:
            copy.wait()
        for copy in remote:
            copy.wait_send()

    anywhere = pl.BlockSpec(memory_space=pl.ANY)
    vmem = pl.BlockSpec(memory_space=pltpu.VMEM)
    smem = pl.BlockSpec(memory_space=pltpu.SMEM)
    act = jax.ShapeDtypeStruct((slots, width), BF16)
    state = jax.ShapeDtypeStruct((users, heads, HEAD, HEAD), F32)
    tile = pltpu.VMEM((users, part, width), BF16)
    return pl.pallas_call(
        body,
        out_shape=(
            act,
            act,
            act,
            act,
            state,
            state,
            jax.ShapeDtypeStruct((2, heads, HEAD, HEAD), BF16),
        ),
        in_specs=[vmem, smem, smem] + [anywhere] * 4,
        out_specs=(anywhere,) * 4 + (vmem,) * 3,
        scratch_shapes=[
            tile,
            tile,
            pltpu.VMEM((3, width, width), BF16),
            pltpu.VMEM((slots, width), BF16),
            tile,
            tile,
            tile,
            pltpu.VMEM((2, heads, HEAD, HEAD), F32),
            pltpu.SemaphoreType.DMA((users - 1,)),
            pltpu.SemaphoreType.DMA((users - 1,)),
            pltpu.SemaphoreType.DMA((5,)),
            pltpu.SemaphoreType.DMA((users, 4)),
        ],
        compiler_params=pltpu.CompilerParams(
            collective_id=0, has_side_effects=True, vmem_limit_bytes=VMEM_LIMIT
        ),
        cost_estimate=cost(6 * slots * width * width, 18 * slots * width),
    )(events, source, filled, cot, *weights)


def gradients(q, k, v, cot, hist, kvp, qdp, st, users, shards, scale, factor):
    slots, width = q.shape
    heads = width // HEAD
    pairs = width // PAIR
    nwin = slots // WINDOW
    per_window = users // nwin
    chips = shards // 2
    half = heads // 2
    groups = users * chips
    own = width // (2 * groups)
    mid = WINDOW // 2

    def body(q_h, k_h, v_h, o_h, hist_h, kvp_h, qdp_h, st_ref, *refs):
        gq_o, gk_o, gv_o, sum_o = refs[:4]
        qs, ks, vs, os, hs, kvs, qds, oth, mine, rk, rq, tot, sums, theirs, states = refs[4:19]
        inner, gs, ht, acc, keep, send, got = refs[19:26]
        in_sem, far_sem, rk_sem, rq_sem, sk_sem, sq_sem, out_sem, ss_sem, gr_sem, so_sem = refs[26:]
        me = lax.axis_index("user")
        place = lax.axis_index("seq")
        core = place % 2
        z = place // 2
        mate = {"seq": place + 1 - 2 * core}

        def chip(by):
            return {"seq": ((z + by + chips) % chips) * 2 + core}

        loads = []
        for w in range(nwin):
            rows = pl.ds(w * WINDOW, WINDOW)
            loads.append(
                [
                    pltpu.make_async_copy(a.at[rows], b.at[rows], in_sem.at[w, n])
                    for n, (a, b) in enumerate(((q_h, qs), (k_h, ks), (v_h, vs), (o_h, os)))
                ]
            )
            for load in loads[-1]:
                load.start()
        late = [
            pltpu.make_async_copy(a, b, in_sem.at[nwin, n])
            for n, (a, b) in enumerate(((hist_h, hs), (kvp_h, kvs), (qdp_h, qds)))
        ]
        for load in late:
            load.start()

        barrier = pltpu.get_barrier_semaphore()
        pl.semaphore_signal(barrier, inc=1, device_id=mate, device_id_type=MESH)
        for j in range(1, chips):
            pl.semaphore_signal(barrier, inc=1, device_id=chip(j), device_id_type=MESH)
        pl.semaphore_wait(barrier, chips)
        swap_in = pltpu.make_async_remote_copy(
            src_ref=st_ref,
            dst_ref=oth,
            send_sem=far_sem.at[0],
            recv_sem=far_sem.at[1],
            device_id=mate,
            device_id_type=MESH,
        )
        swap_in.start()

        row = lax.broadcasted_iota(jnp.int32, (mid, mid), 0)
        lane = lax.broadcasted_iota(jnp.int32, (mid, mid), 1)

        def masked(x, keep_it):
            return jnp.where(keep_it, x, 0.0).astype(BF16)

        def inside(w, first, last):
            low = lane <= row
            high = lane >= row
            top, low_half = pl.ds(w * WINDOW, mid), pl.ds(w * WINDOW + mid, mid)

            def step(n, carry):
                cols = pl.ds(pl.multiple_of(n * HEAD, HEAD), HEAD)
                q0, q1 = qs[top, cols], qs[low_half, cols]
                k0, k1 = ks[top, cols], ks[low_half, cols]
                v0, v1 = vs[top, cols], vs[low_half, cols]
                o0, o1 = os[top, cols], os[low_half, cols]
                m00 = masked(mm_nt(o0, v0), low)
                m10 = mm_nt(o1, v0).astype(BF16)
                m11 = masked(mm_nt(o1, v1), low)
                t00 = masked(mm_nt(v0, o0), high)
                t01 = mm_nt(v0, o1).astype(BF16)
                t11 = masked(mm_nt(v1, o1), high)
                s00 = masked(mm_nt(k0, q0), high)
                s01 = mm_nt(k0, q1).astype(BF16)
                s11 = masked(mm_nt(k1, q1), high)
                inner[0, top, cols] = mm(m00, k0)
                inner[0, low_half, cols] = mm(m10, k0) + mm(m11, k1)
                inner[1, top, cols] = mm(t00, q0) + mm(t01, q1)
                inner[1, low_half, cols] = mm(t11, q1)
                inner[2, top, cols] = mm(s00, o0) + mm(s01, o1)
                inner[2, low_half, cols] = mm(s11, o1)
                return carry

            lax.fori_loop(first, last, step, 0)

        for load in loads[0]:
            load.wait()
        inside(0, 0, heads // 4)
        swap_in.wait()
        mine_heads = pl.ds(core * half, half)
        for n in range(2):
            both = st_ref[n, mine_heads].astype(F32) + oth[n, mine_heads].astype(F32)
            mine[n] = both.astype(BF16)
        inside(0, heads // 4, heads // 2)

        def far(kind, j):
            slots_in, send_s, recv_s = ((rk, sk_sem, rk_sem), (rq, sq_sem, rq_sem))[kind]
            return pltpu.make_async_remote_copy(
                src_ref=mine.at[kind],
                dst_ref=slots_in.at[j - 1],
                send_sem=send_s.at[j - 1],
                recv_sem=recv_s.at[j - 1],
                device_id=chip(j if kind == 0 else -j),
                device_id_type=MESH,
            )

        for j in range(1, chips):
            pl.when(z + j < chips)(lambda j=j: far(0, j).start())
            pl.when(z >= j)(lambda j=j: far(1, j).start())
        inside(0, heads // 2, heads)
        for w in range(1, nwin):
            for load in loads[w]:
                load.wait()
            inside(w, 0, heads - heads // 4 if w == nwin - 1 else heads)
        tot[...] = jnp.zeros_like(tot)
        for j in range(1, chips):

            @pl.when(z >= j)
            def _(j=j):
                far(0, j).wait_recv()
                tot[0] += rk[j - 1].astype(F32)
                far(1, j).wait_send()

            @pl.when(z + j < chips)
            def _(j=j):
                far(1, j).wait_recv()
                tot[1] += rq[j - 1].astype(F32)
                far(0, j).wait_send()

        sums[...] = tot[...].astype(BF16)
        inside(nwin - 1, heads - heads // 4, heads)
        swap_out = pltpu.make_async_remote_copy(
            src_ref=sums,
            dst_ref=theirs,
            send_sem=far_sem.at[2],
            recv_sem=far_sem.at[3],
            device_id=mate,
            device_id_type=MESH,
        )
        swap_out.start()
        for load in late:
            load.wait()
        ht[...] = hs[...].T
        swap_out.wait()
        other_heads = pl.ds((1 - core) * half, half)
        later_core = jnp.where(core == 1, 1.0, 0.0)
        for n in range(2):
            states[n, mine_heads] = tot[n]
            states[n, other_heads] = theirs[n].astype(F32)
            on = later_core if n == 0 else 1.0 - later_core
            states[n] = states[n] + on * oth[n].astype(F32)

        def push(c):
            return pltpu.make_async_remote_copy(
                src_ref=send.at[c],
                dst_ref=got.at[c],
                send_sem=ss_sem.at[c],
                recv_sem=gr_sem.at[c],
                device_id=mate,
                device_id_type=MESH,
            )

        def finish(c, carry):
            pl.when(c > 0)(lambda: push(c - 1).start())
            cols = pl.ds(pl.multiple_of(c * PAIR, PAIR), PAIR)
            for w in range(nwin):
                rows = pl.ds(w * WINDOW, WINDOW)
                for i in range(2):
                    head = 2 * c + i
                    at = pl.ds(pl.multiple_of(head * HEAD, HEAD), HEAD)
                    bef, aft = states[0, head], states[1, head]
                    for j in range(users):
                        its = jnp.bitwise_xor(me, j) // per_window
                        bef = bef + jnp.where(its < w, 1.0, 0.0) * kvs[j, head]
                        aft = aft + jnp.where(its > w, 1.0, 0.0) * qds[j, head]
                    bef, aft = bef.astype(BF16), aft.astype(BF16)
                    gq = inner[0, rows, at] + mm_nt(os[rows, at], bef)
                    gk = inner[1, rows, at] + mm_nt(vs[rows, at], aft)
                    gv = inner[2, rows, at] + mm(ks[rows, at], aft)
                    for n, g in enumerate((gq, gk, gv)):
                        gs[n, rows, at] = (g * scale).astype(BF16)
            for n in range(3):
                acc[...] = mm(ht[...], gs[n, :, cols]) * factor
                for g in range(groups):
                    at = pl.multiple_of(g * 2 * own + core * own, 8)
                    away = pl.multiple_of(g * 2 * own + (1 - core) * own, 8)
                    keep[c, n, g] = acc[pl.ds(at, own), :].astype(BF16)
                    send[c, n, g] = acc[pl.ds(away, own), :].astype(BF16)
            return carry

        lax.fori_loop(0, pairs, finish, 0)
        outs = [
            pltpu.make_async_copy(gs.at[n], g, out_sem.at[n])
            for n, g in enumerate((gq_o, gk_o, gv_o))
        ]
        for copy in outs:
            copy.start()

        def settle(c):
            push(c).wait()
            keep[c] = (keep[c].astype(F32) + got[c].astype(F32)).astype(BF16)
            return pltpu.make_async_copy(keep.at[c], sum_o.at[c], so_sem.at[c])

        for c in range(pairs):
            if c == min(1, pairs - 1):
                push(pairs - 1).start()
            settled = settle(c)
            settled.start()
            outs.append(settled)
        for copy in outs:
            copy.wait()

    anywhere = pl.BlockSpec(memory_space=pl.ANY)
    act = jax.ShapeDtypeStruct((slots, width), BF16)
    whole = pltpu.VMEM((slots, width), BF16)
    piece = pltpu.VMEM((users, heads, HEAD, HEAD), F32)
    pack = (pairs, 3, groups, own, PAIR)
    state = (2, heads, HEAD, HEAD)
    part = (2, half, HEAD, HEAD)
    one = pltpu.VMEM((chips - 1, half, HEAD, HEAD), BF16)
    sem = pltpu.SemaphoreType.DMA
    return pl.pallas_call(
        body,
        out_shape=(act, act, act, jax.ShapeDtypeStruct(pack, BF16)),
        in_specs=[anywhere] * 7 + [pl.BlockSpec(memory_space=pltpu.VMEM)],
        out_specs=(anywhere,) * 4,
        scratch_shapes=[
            whole,
            whole,
            whole,
            whole,
            whole,
            piece,
            piece,
            pltpu.VMEM(state, BF16),
            pltpu.VMEM(part, BF16),
            one,
            one,
            pltpu.VMEM(part, F32),
            pltpu.VMEM(part, BF16),
            pltpu.VMEM(part, BF16),
            pltpu.VMEM(state, F32),
            pltpu.VMEM((3, slots, width), F32),
            pltpu.VMEM((3, slots, width), BF16),
            pltpu.VMEM((width, slots), BF16),
            pltpu.VMEM((width, PAIR), F32),
            pltpu.VMEM(pack, BF16),
            pltpu.VMEM(pack, BF16),
            pltpu.VMEM(pack, BF16),
            sem((nwin + 1, 4)),
            sem((4,)),
            sem((chips - 1,)),
            sem((chips - 1,)),
            sem((chips - 1,)),
            sem((chips - 1,)),
            sem((3,)),
            sem((pairs,)),
            sem((pairs,)),
            sem((pairs,)),
        ],
        compiler_params=pltpu.CompilerParams(
            collective_id=1, has_side_effects=True, vmem_limit_bytes=VMEM_LIMIT
        ),
        cost_estimate=cost(12 * slots * width * width, 30 * slots * width),
    )(q, k, v, cot, hist, kvp, qdp, st)


def tail(home, sums, grads, weights, users, shards, blocks):
    slots, width = grads[0].shape
    part = slots // users
    capacity = part // EVB
    chips = shards // 2
    pairs, own, lanes = sums.shape[0], sums.shape[-2], sums.shape[-1]
    side = pairs // 2
    cut = width // 2

    def body(home_ref, sums_h, gq_h, gk_h, gv_h, wq_h, wk_h, wv_h, out, share, *refs):
        gs, ws, ss, hb, ret, first, keep, give, second, zs, rz = refs[:11]
        in_sem, s1, r1, s2, r2, sz, rzs, sa, ra = refs[11:]
        me = lax.axis_index("user")
        place = lax.axis_index("seq")
        core = place % 2
        z = place // 2
        bits = (me % 2, me // 2)

        def user(j):
            return {"user": jnp.bitwise_xor(me, j)}

        def chip(j):
            return {"seq": jnp.bitwise_xor(z, j) * 2 + core}

        loads = []
        for n, (a, b) in enumerate(zip((gq_h, gk_h, gv_h), (wq_h, wk_h, wv_h))):
            loads.append(pltpu.make_async_copy(a, gs.at[n], in_sem.at[n]))
            loads.append(pltpu.make_async_copy(b, ws.at[n], in_sem.at[3 + n]))
        loads.append(pltpu.make_async_copy(sums_h, ss, in_sem.at[6]))
        for load in loads:
            load.start()
        barrier = pltpu.get_barrier_semaphore()
        for j in range(1, users):
            pl.semaphore_signal(barrier, inc=1, device_id=user(j), device_id_type=MESH)
        for j in range(1, chips):
            pl.semaphore_signal(barrier, inc=1, device_id=chip(j), device_id_type=MESH)
        pl.semaphore_wait(barrier, users + chips - 2)

        def remote(src, dst, send_sem, recv_sem, where):
            return pltpu.make_async_remote_copy(
                src_ref=src,
                dst_ref=dst,
                send_sem=send_sem,
                recv_sem=recv_sem,
                device_id=where,
                device_id_type=MESH,
            )

        half = (pl.ds(0, side), pl.ds(side, side))
        one = []
        for n in range(2):
            away = 1 - bits[n]
            src = sums_h.at[half[0], :, :, away] if n == 0 else sums_h.at[half[1], :, away]
            one.append(remote(src, first.at[n], s1.at[n], r1.at[n], user(1 + n)))
            one[-1].start()

        def back(j, c):
            at = (pl.ds(j * capacity, capacity), slice(None), pl.ds(c * cut, cut))
            return remote(hb.at[at], ret.at[at], sa.at[j - 1, c], ra.at[j - 1, c], user(j))

        for load in loads[:-1]:
            load.wait()
        order = [j for j in (1, 2) if j < users] + list(range(3, users)) + [0]
        pending = None
        for j in order:
            rows = pl.ds(pl.multiple_of(jnp.bitwise_xor(me, j) * part, part), part)
            for c in range(2):
                cols = pl.ds(c * cut, cut)
                value = mm_nt(gs[0, rows, :], ws[0, cols, :])
                value = value + mm_nt(gs[1, rows, :], ws[1, cols, :])
                value = (value + mm_nt(gs[2, rows, :], ws[2, cols, :])).astype(BF16)
                into = hb if j else ret
                for i in range(capacity):
                    into[j * capacity + i, :, cols] = value[i * EVB : (i + 1) * EVB]
                if pending is not None:
                    pending.start()
                pending = back(j, c) if j in (1, 2) else None
        loads[-1].wait()

        two = []
        for n in range(2):
            one[n].wait()
            at, nxt = bits[n], bits[1 - n]
            if n == 0:
                gone, stay = ss[half[0], :, 1 - nxt, at], ss[half[0], :, nxt, at]
            else:
                gone, stay = ss[half[1], :, at, 1 - nxt], ss[half[1], :, at, nxt]
            give[n] = add(gone, first[n, :, :, 1 - nxt]).astype(BF16)
            keep[n] = add(stay, first[n, :, :, nxt])
            two.append(remote(give.at[n], second.at[n], s2.at[n], r2.at[n], user(2 - n)))
            two[-1].start()
        for j in range(3, users):
            for c in range(2):
                back(j, c).start()
        for n in range(2):
            two[n].wait()
            keep[n] = keep[n] + second[n].astype(F32)
        far = []
        for j in range(1, chips):
            to = jnp.bitwise_xor(z, j)
            for n in range(2):
                zs[j - 1, half[n]] = keep[n, :, :, to].astype(BF16)
        for n in range(2):
            share[half[n]] = keep[n, :, :, z]
        for j in range(1, chips):
            far.append(remote(zs.at[j - 1], rz.at[j - 1], sz.at[j - 1], rzs.at[j - 1], chip(j)))
            far[-1].start()
        for copy in far:
            copy.wait()
        total = share[...]
        for j in range(1, chips):
            total = total + rz[j - 1].astype(F32)
        share[...] = total
        for j in range(1, users):
            for c in range(2):
                back(j, c).wait()
        for b in range(blocks):
            out[b] = ret[home_ref[b]]

    anywhere = pl.BlockSpec(memory_space=pl.ANY)
    vmem = pl.BlockSpec(memory_space=pltpu.VMEM)
    sem = pltpu.SemaphoreType.DMA
    rows = (users * capacity, EVB, width)
    quarter = (2, side, 3, chips, own, lanes)
    return pl.pallas_call(
        body,
        out_shape=(
            jax.ShapeDtypeStruct((blocks, EVB, width), BF16),
            jax.ShapeDtypeStruct((pairs, 3, own, lanes), F32),
        ),
        in_specs=[pl.BlockSpec(memory_space=pltpu.SMEM)] + [anywhere] * 7,
        out_specs=(vmem, vmem),
        scratch_shapes=[
            pltpu.VMEM((3, slots, width), BF16),
            pltpu.VMEM((3, width, width), BF16),
            pltpu.VMEM(sums.shape, BF16),
            pltpu.VMEM(rows, BF16),
            pltpu.VMEM(rows, BF16),
            pltpu.VMEM((2, side, 3, 2, chips, own, lanes), BF16),
            pltpu.VMEM(quarter, F32),
            pltpu.VMEM(quarter, BF16),
            pltpu.VMEM(quarter, BF16),
            pltpu.VMEM((chips - 1, pairs, 3, own, lanes), BF16),
            pltpu.VMEM((chips - 1, pairs, 3, own, lanes), BF16),
            sem((7,)),
            sem((2,)),
            sem((2,)),
            sem((2,)),
            sem((2,)),
            sem((chips - 1,)),
            sem((chips - 1,)),
            sem((users - 1, 2)),
            sem((users - 1, 2)),
        ],
        compiler_params=pltpu.CompilerParams(
            collective_id=2, has_side_effects=True, vmem_limit_bytes=VMEM_LIMIT
        ),
        cost_estimate=cost(6 * slots * width * width, 20 * slots * width),
    )(home, sums, *grads, *weights)


def add(*terms):
    return functools.reduce(jnp.add, [t.astype(F32) for t in terms])


def local(events, routing, grad_out, w_query, w_key, w_value):
    users = lax.axis_size("user")
    shards = lax.axis_size("seq")
    me = lax.axis_index("user").astype(jnp.int32)
    blocks = routing.shape[0]
    width = events.shape[1]
    slots = grad_out.shape[1]
    capacity = slots // (users * EVB)
    route = routing[:, 0]

    order = lax.iota(jnp.int32, blocks)
    same = (route[None, :] == route[:, None]) & (order[None, :] < order[:, None])
    rank = jnp.sum(same.astype(jnp.int32), axis=1)
    home = jnp.bitwise_xor(route, me) * capacity + rank
    slot = lax.iota(jnp.int32, users * capacity)
    hit = home[None, :] == slot[:, None]
    source = jnp.sum(jnp.where(hit, order[None, :], 0), axis=1)
    filled = jnp.sum(hit.astype(jnp.int32), axis=1)
    cot = grad_out[0]
    weights = (w_query, w_key, w_value)
    hist, q, k, v, kvp, qdp, state = project(
        events.reshape(blocks, EVB, width), source, filled, cot, weights, users
    )
    scale = 1.0 / math.sqrt(HEAD * slots * shards)
    factor = 1.0 / math.sqrt(users * slots * shards)
    gq, gk, gv, sums = gradients(
        q, k, v, cot, hist, kvp, qdp, state, users, shards, scale, factor
    )
    sums = sums.reshape(sums.shape[:2] + (users // 2, 2, shards // 2) + sums.shape[3:])
    grad_events, shares = tail(home, sums, (gq, gk, gv), weights, users, shards, blocks)
    pairs, _, own, lanes = shares.shape
    shares = jnp.transpose(shares, (1, 2, 0, 3)).reshape(3, own, pairs * lanes)
    return (grad_events.reshape(blocks * EVB, width), shares[0], shares[1], shares[2])


def solution(mesh):
    placed = (
        P(("user", "seq"), None),
        P(("user", "seq"), None),
        P("user", "seq", None),
        P(),
        P(),
        P(),
    )
    return jax.shard_map(
        local,
        mesh=mesh,
        in_specs=placed,
        out_specs=(P(("user", "seq"), None),) * 4,
        check_vma=False,
    )
```
